32 devices in a mesh: sec: 4 (over y, x), tile: 8 (over z, core).
Axes of the slice: x: 2, y: 2, z: 4, core: 2. Of those that a mesh axis runs over, the one named last changes fastest.
Arguments:
- displacement: float32 [2, 16, 256, 256], P(None, 'sec', 'tile'), may hold values from -3 to 3
- coupling: float32 [4, 16, 256, 256], P(None, 'sec', 'tile'), may hold values from 0.1 to 1
- matches: float32 [4, 2, 16, 256, 256], P(None, None, 'sec', 'tile'), may hold values from -3 to 3
- step_sizes: float32 [2, 8], replicated, may hold values from 0.1 to 0.35
- restarts: int32 [2, 8], replicated, may hold values 0 or 1
- images: float32 [4, 64, 256, 256], P('sec', 'tile'), may hold values from 0 to 1
- block_anchor: int32 [4, 64], P('sec', 'tile'), may hold values from 0 to 32767
- block_dest: int32 [4, 64, 1], P('sec', 'tile'), may hold values from 0 to 7; in each aligned block of 8 rows (0 to 7, 8 to 15, ..., all dimensions but the last counted through in order) at most 2 rows name the same one
- block_slot: int32 [4, 64], P('sec', 'tile'), may hold values from 0 to 1
- block_offset: int32 [4, 64, 2], P('sec', 'tile'), may hold values from 0 to 128
- block_count: int32 [4, 8], P('sec', 'tile'), may hold values from 6 to 8, as said below
Outputs:
- aligned: float32 [2, 16, 256, 256], P(None, 'sec', 'tile')
- spans: float32 [64, 384, 384], P(('sec', 'tile'))
The draws below stay inside these ranges and needn't reach their ends.
Inputs may be any that keep to these rules, and one draw needn't show every extreme that they name: `block_dest`: no tile index is named by more than 2 of the block slots of one device, and 2 is reached. `block_count`: some device uses all 8 slots.
All inputs are finite; a program needn't handle non-finite values.
Results may differ from the reference program's by a relative error of at most 0.0003.
Values sent between devices are 32-bit elements; how exact they have to be, the bound alone decides.
A program may use at most 128 MiB of HBM per device.

```python
import math
import jax
import jax.numpy as jnp
import numpy as np
from jax import lax

SEC_DEV = 4
GRID = 256
OUTER = 2
FIRE_STEPS = 8
BLK_DEV = 8
BPP = 256
CH = 384
SPAN_DEV = 2
SECTIONS = 16
ROWS_DEV = 32
BLOCK_ROWS = 64
CAP = 2
N_SEC = 4
N_TILE = 8


def draw_block_count(key, part):
    lowest = 3 * BLK_DEV // 4
    counts = jax.random.randint(jax.random.fold_in(key, 11), (N_SEC * N_TILE,), lowest, BLK_DEV + 1)
    forced = jax.random.randint(jax.random.fold_in(key, 12), (), 0, N_SEC * N_TILE)
    counts = jnp.where(jnp.arange(N_SEC * N_TILE) == forced, BLK_DEV, counts)
    return counts.reshape(N_SEC, N_TILE).astype(jnp.int32)


def block_field(values):
    return jnp.repeat(jnp.repeat(values, SEC_DEV, axis=0), ROWS_DEV, axis=1)


def draw_coupling(key, part):
    spread = jax.random.uniform(jax.random.fold_in(key, 21), (N_SEC, N_TILE), jnp.float32, 0.0, 1.0)
    spread_full = block_field(spread)
    base = jax.random.uniform(jax.random.fold_in(key, 22), (4, SECTIONS, GRID, GRID), jnp.float32, 0.0, 1.0)
    exponent = -1.0 + 0.3 * base + 0.7 * spread_full[None, :, :, None]
    return jnp.clip(jnp.power(10.0, exponent), 0.1, 1.0).astype(jnp.float32)


def draw_matches(key, part):
    level = jax.random.uniform(jax.random.fold_in(key, 31), (N_SEC, N_TILE), jnp.float32, 0.0, 1.0)
    scale_full = block_field(jnp.power(10.0, level - 0.5))
    noise = jax.random.normal(jax.random.fold_in(key, 32), (4, 2, SECTIONS, GRID, GRID), jnp.float32)
    values = 0.5 * noise * scale_full[None, None, :, :, None]
    return jnp.clip(values, -3.0, 3.0).astype(jnp.float32)


def plant(result, stream_key, smallest, top_value):
    index_at = [jax.random.randint(jax.random.fold_in(stream_key, axis), (), 0, length) for axis, length in enumerate(result.shape)]
    main_axis = result.shape.index(max(result.shape))
    beside = index_at[:main_axis] + [(index_at[main_axis] + 1) % result.shape[main_axis]] + index_at[main_axis + 1:]
    return result.at[tuple(index_at)].set(smallest).at[tuple(beside)].set(top_value)


def steps_of(key, extent, pieces, smallest, largest):
    loudness = 1.0
    for axis_at, blocks in pieces:
        heights = jax.random.uniform(jax.random.fold_in(jax.random.fold_in(key, 6), axis_at), (blocks,), jnp.float32, smallest / len(pieces), largest / len(pieces))
        loudness = loudness * jnp.repeat(jnp.exp(heights), extent[axis_at] // blocks).reshape((-1,) + (1,) * (len(extent) - 1 - axis_at))
    return loudness


def assign_block(key, own, number, rows, amount, top, most, lean):
    ranking = jax.random.permutation(key, amount)
    crowded, common = load_shares(amount, rows * top, most, lean, True), load_shares(amount, rows * top, most, lean, False)
    places = jnp.arange(amount)

    def named(tallies, offset_by):
        used = int((tallies > 0).sum())
        fixed = max(1, used // 4)
        moved = fixed + (places - fixed + offset_by * (used - fixed)) % max(1, amount - fixed)
        return jnp.zeros((amount,), jnp.int32).at[ranking[jnp.where(places < fixed, places, moved)]].set(jnp.asarray(tallies, jnp.int32))

    tallies = jnp.where(number % 4 == 0, named(crowded, number // 4), named(common, number - number // 4 - 1))
    mixed = jax.random.permutation(jax.random.fold_in(own, 3), amount)
    source_of, receiver = mixed[0:amount // 2 * 2:2], mixed[1:amount // 2 * 2:2]
    room = jnp.minimum(tallies[source_of] - 1, most - tallies[receiver]) // 2
    room = jnp.where((source_of == ranking[0]) | (receiver == ranking[0]) | (tallies[receiver] == 0), 0, jnp.maximum(room, 0))
    moved = jax.random.randint(jax.random.fold_in(own, 4), (amount // 2,), 0, 1 << 20) % (room + 1)
    tallies = tallies.at[source_of].add(-moved).at[receiver].add(moved)
    labels = jnp.searchsorted(jnp.cumsum(tallies), jnp.arange(rows * top), side="right").astype(jnp.int32)
    listing = labels.reshape(top, rows).T
    listing = listing[jax.random.permutation(jax.random.fold_in(own, 1), rows)]
    offset_by = jax.random.randint(jax.random.fold_in(own, 2), (rows, 1), 0, top)
    return jnp.take_along_axis(listing, (jnp.arange(top)[None, :] + offset_by) % top, axis=1)


def load_shares(amount, total, bound, lean, full):
    weights = [(1 << 20) // math.isqrt(rank ** lean) + 1 for rank in range(1, amount + 1)]
    largest = bound if full else min(bound, max(-(-total // amount), total * weights[0] // sum(weights)))
    least = 1 if total - largest >= amount - 1 else 0
    given, spare = [largest] + [least] * (amount - 1), total - largest - least * (amount - 1)
    while spare > 0:
        free = [i for i in range(1, amount) if given[i] < largest] or [i for i in range(1, amount) if given[i] < bound]
        whole, left = sum([weights[i] for i in free]), spare
        for i in free:
            extra = min(bound - given[i], max(1, left * weights[i] // whole), spare)
            given[i] = given[i] + extra
            spare = spare - extra
    return np.array(given)


def normal_values(own_key, shape, scale, most, split=(), kind=jnp.bfloat16):
    loudness = steps_of(own_key, shape, split, -0.22, 0.18) if split else 1.0
    values = jax.random.normal(own_key, shape, jnp.float32) * scale * loudness
    return jnp.minimum(jnp.maximum(values, -most), most).astype(kind)


def setup_inputs(seed: int = 0) -> dict:
    keys = jax.random.split(jax.random.key(seed), 12)
    displacement = normal_values(keys[0], (2, SECTIONS, GRID, GRID), 0.5, 3.0, ((1, 4), (2, 8)), jnp.float32)
    coupling = draw_coupling(jax.random.fold_in(keys[11], 71), 0)
    matches = draw_matches(jax.random.fold_in(keys[11], 71), 0)
    step_sizes = jnp.clip(jnp.exp(jax.random.uniform(keys[3], (OUTER, FIRE_STEPS), jnp.float32, math.log(0.1), math.log(0.35))), 0.1, 0.35)
    restarts = plant((jax.random.randint(keys[4], (OUTER, FIRE_STEPS), 0, 4) < 1).astype(jnp.int32), jax.random.fold_in(keys[4], 1), 0, 1)
    images = jnp.clip(1.0 * jax.random.uniform(keys[5], (N_SEC, BLOCK_ROWS, BPP, BPP), jnp.float32) ** steps_of(keys[5], (N_SEC, BLOCK_ROWS, BPP, BPP), ((0, 4), (1, 8)), -0.2, 0.2), 0.0, 1.0)
    block_anchor = plant(jax.random.randint(keys[6], (N_SEC, BLOCK_ROWS), 0, SEC_DEV * ROWS_DEV * GRID), jax.random.fold_in(keys[6], 1), 0, (SEC_DEV * ROWS_DEV * GRID) - 1).astype(jnp.int32)
    block_dest_keys = jax.random.split(jax.random.fold_in(keys[7], 1), N_SEC * BLOCK_ROWS // BLK_DEV)
    block_dest_turns = jax.random.permutation(jax.random.fold_in(keys[7], 3), N_SEC * BLOCK_ROWS // BLK_DEV)
    block_dest = jax.vmap(lambda own, number: assign_block(jax.random.fold_in(keys[7], 2), own, number, BLK_DEV, N_TILE, 1, CAP, 2))(block_dest_keys, block_dest_turns).reshape((N_SEC, BLOCK_ROWS, 1))
    block_slot = plant(jax.random.randint(keys[8], (N_SEC, BLOCK_ROWS), 0, SPAN_DEV), jax.random.fold_in(keys[8], 1), 0, SPAN_DEV - 1).astype(jnp.int32)
    block_offset = plant(jax.random.randint(keys[9], (N_SEC, BLOCK_ROWS, 2), 0, CH - BPP + 1), jax.random.fold_in(keys[9], 1), 0, CH - BPP).astype(jnp.int32)
    block_count = draw_block_count(jax.random.fold_in(keys[11], 71), 0)
    return dict(displacement=displacement, coupling=coupling, matches=matches, step_sizes=step_sizes, restarts=restarts, images=images, block_anchor=block_anchor, block_dest=block_dest, block_slot=block_slot, block_offset=block_offset, block_count=block_count)


STIFFNESS = 1.0
MIXING = 0.1
EPSILON = 1e-06
SPEED_CAP = 0.1
PRECISE = lax.Precision.HIGHEST

def laplace(field):
    padded = jnp.pad(field, ((0, 0), (0, 0), (1, 1), (1, 1)))
    return padded[:, :, 2:, 1:-1] + padded[:, :, :-2, 1:-1] + padded[:, :, 1:-1, 2:] + padded[:, :, 1:-1, :-2] - 4.0 * field

def forces(current, refer, coupling, matches):
    summed = STIFFNESS * laplace(current - refer)
    sections_all = current.shape[1]
    padded = jnp.pad(current, ((0, 0), (2, 2), (0, 0), (0, 0)))
    section = jnp.arange(sections_all)
    for which_k, reach in enumerate((-2, -1, 1, 2)):
        beside = padded[:, 2 + reach:2 + reach + sections_all]
        usable = ((section + reach >= 0) & (section + reach < sections_all)).astype(jnp.float32)
        summed = summed + usable[None, :, None, None] * coupling[which_k][None] * (beside + matches[which_k] - current)
    return summed

def hat_rows(shift, size, source):
    row_pos = jnp.arange(size).astype(jnp.float32)[None, :, None]
    src_pos = jnp.arange(source).astype(jnp.float32)[None, None, :]
    return jnp.maximum(0.0, 1.0 - jnp.abs(row_pos - src_pos - shift[:, None, None]))

def warp_blocks(blocks_in, shift_y, shift_x):
    row_hats = hat_rows(shift_y, CH, BPP)
    col_hats = hat_rows(shift_x, CH, BPP)
    halfway = jnp.einsum('bij,bkj->bik', blocks_in, col_hats, precision=PRECISE)
    return jnp.einsum('bri,bik->brk', row_hats, halfway, precision=PRECISE)

def reference(displacement, coupling, matches, step_sizes, restarts, images, block_anchor, block_dest, block_slot, block_offset, block_count):
    current = displacement
    refer = displacement
    velocity = jnp.zeros_like(displacement)
    node_total = 2.0 * current.shape[1] * current.shape[2] * current.shape[3]
    for outer_step in range(OUTER):
        for inner_step in range(FIRE_STEPS):
            delta = step_sizes[outer_step, inner_step]
            push = forces(current, refer, coupling, matches)
            velocity = velocity + delta * push
            speed_sq = jnp.sum(velocity * velocity)
            push_sq = jnp.sum(push * push)
            ratio = jnp.sqrt(speed_sq + EPSILON) / jnp.sqrt(push_sq + EPSILON)
            limit = jnp.minimum(1.0, SPEED_CAP / jnp.sqrt(speed_sq / node_total + EPSILON))
            retain = 1.0 - restarts[outer_step, inner_step].astype(jnp.float32)
            velocity = limit * retain * ((1.0 - MIXING) * velocity + MIXING * ratio * push)
            current = current + delta * velocity
        refer = current
        velocity = jnp.zeros_like(current)

    def render_group(group):
        block_ids = jnp.arange(N_TILE * BLK_DEV)
        tile_of = block_ids // BLK_DEV
        usable = (block_ids % BLK_DEV < block_count[group][tile_of]).astype(jnp.float32)
        anchor = block_anchor[group]
        local_sec = anchor // (ROWS_DEV * GRID)
        local_row = anchor // GRID % ROWS_DEV
        column = anchor % GRID
        sec_all = (group * SEC_DEV + local_sec).astype(jnp.int32)
        row_all = (tile_of * ROWS_DEV + local_row).astype(jnp.int32)
        moved = current[:, sec_all, row_all, column.astype(jnp.int32)]
        offsets = block_offset[group].astype(jnp.float32)
        drawn = warp_blocks(images[group], offsets[:, 0] + moved[0], offsets[:, 1] + moved[1])
        target = block_dest[group][:, 0] * SPAN_DEV + block_slot[group]
        select = (target[:, None] == jnp.arange(N_TILE * SPAN_DEV)[None, :]).astype(jnp.float32) * usable[:, None]
        return jnp.einsum('bc,brk->crk', select, drawn, precision=PRECISE)
    rendered = lax.map(render_group, jnp.arange(N_SEC))
    spans = rendered.reshape(N_SEC * N_TILE * SPAN_DEV, CH, CH)
    return (current, spans)
```

```python
import functools

import jax
import jax.numpy as jnp
from jax import lax
from jax.experimental import pallas as pl
from jax.experimental.pallas import tpu as pltpu
from jax.sharding import PartitionSpec as P


OUTER = 2
FIRE_STEPS = 8
CH = 384
SPAN_DEV = 2
REACHES = (-2, -1, 1, 2)

MIXING = 0.1
EPSILON = 1e-06
SPEED_CAP = 0.1
HALF = 8.0
MESH = pl.DeviceIdType.MESH
LANES = 128


def pair_order(index):
    odd = (index // 2) % 2
    return index + odd * (1 - 2 * (index % 2))


def fire_kernel(
    n_sec, n_tile, steps, keep, packed, out,
    fields, disp, basis, diag, edge_up, edge_dn, halo_up, halo_dn, rows, gram, from_sec, from_tile,
    in_send, in_recv, up_send, up_recv, dn_send, dn_recv,
    gs_send, gs_recv, gt_send, gt_recv, out_send, out_recv,
):
    s, t = lax.axis_index("sec"), lax.axis_index("tile")
    own, n_rows, width = packed.shape[1], packed.shape[3], packed.shape[4]
    sections = own * n_sec
    node_total = float(2 * sections * width * width)

    def place(which, tile):
        order = pair_order(which)
        return order + (tile % 2) * (n_sec - 1 - 2 * order)

    q = place(s, t)
    first = jnp.logical_and(q == 0, t == 0)
    last = jnp.logical_and(q == n_sec - 1, t == n_tile - 1)

    def holder(position):
        tile = position // n_sec
        at = position % n_sec
        return pair_order(at + (tile % 2) * (n_sec - 1 - 2 * at)), tile

    position = t * n_sec + q
    above = holder(lax.rem(position - 1 + n_sec * n_tile, n_sec * n_tile))
    below = holder(lax.rem(position + 1, n_sec * n_tile))

    barrier = pltpu.get_barrier_semaphore()
    for j in range(1, n_sec):
        pl.semaphore_signal(barrier, inc=1, device_id=(lax.rem(s + j, n_sec), t), device_id_type=MESH)
    for j in range(1, n_tile):
        pl.semaphore_signal(barrier, inc=1, device_id=(s, lax.rem(t + j, n_tile)), device_id_type=MESH)
    pl.semaphore_wait(barrier, n_sec + n_tile - 2)

    def send_in(j):
        peer = lax.rem(s + j, n_sec)
        return pltpu.make_async_remote_copy(
            src_ref=packed.at[:, :, place(peer, t)], dst_ref=fields.at[:, pl.ds(s * own, own)],
            send_sem=in_send.at[j], recv_sem=in_recv.at[j], device_id=(peer, t), device_id_type=MESH)

    for j in range(1, n_sec):
        send_in(j).start()
    mine = pltpu.make_async_copy(packed.at[:, :, q], fields.at[:, pl.ds(s * own, own)], in_recv.at[0])
    mine.start()
    blank = jnp.zeros((n_rows, width), jnp.float32)
    for c in range(2):
        for i in (0, 1, sections + 2, sections + 3):
            disp[c, i] = blank
            for k in range(FIRE_STEPS + 1):
                basis[k, c, i] = blank
        for i in range(sections):
            basis[0, c, i + 2] = blank

    @pl.when(first)
    def _():
        halo_up[...] = jnp.zeros_like(halo_up)

    @pl.when(last)
    def _():
        halo_dn[...] = jnp.zeros_like(halo_dn)

    rows[...] = jnp.zeros_like(rows)
    mine.wait()
    for j in range(1, n_sec):
        send_in(j).wait()

    for i in range(sections):
        diag[i] = 4.0 + fields[0, i] + fields[1, i] + fields[2, i] + fields[3, i]
        for c in range(2):
            disp[c, i + 2] = fields[6 + c, i]

    column = lax.broadcasted_iota(jnp.int32, (n_rows, width), 1)
    sub = lax.broadcasted_iota(jnp.int32, (8, LANES), 0)
    lane = lax.broadcasted_iota(jnp.int32, (8, LANES), 1)

    def to_up(k):
        return pltpu.make_async_remote_copy(
            src_ref=edge_up.at[k], dst_ref=halo_dn.at[k],
            send_sem=up_send.at[k], recv_sem=up_recv.at[k], device_id=above, device_id_type=MESH)

    def to_dn(k):
        return pltpu.make_async_remote_copy(
            src_ref=edge_dn.at[k], dst_ref=halo_up.at[k],
            send_sem=dn_send.at[k], recv_sem=dn_recv.at[k], device_id=below, device_id_type=MESH)

    def all_sum(outer):
        def over(j, axis):
            if axis == 0:
                peer, land, send, recv = (lax.rem(s + j, n_sec), t), from_sec, gs_send, gs_recv
            else:
                peer, land, send, recv = (s, lax.rem(t + j, n_tile)), from_tile, gt_send, gt_recv
            return pltpu.make_async_remote_copy(
                src_ref=gram.at[outer, axis], dst_ref=land.at[outer, j],
                send_sem=send.at[outer, j], recv_sem=recv.at[outer, j], device_id=peer, device_id_type=MESH)

        total = gram[outer, 0]
        for axis, size, land in ((0, n_sec, from_sec), (1, n_tile, from_tile)):
            if axis == 1:
                gram[outer, 1] = total
            for j in range(1, size):
                over(j, axis).start()
            for j in range(1, size):
                over(j, axis).wait()
            for j in range(1, size):
                total = total + land[outer, j]
        return total

    for outer in range(OUTER):
        for c in range(2):
            for i in range(sections):
                here = disp[c, i + 2]
                push = fields[4 + c, i]
                for which, reach in enumerate(REACHES):
                    push = push + fields[which, i] * (disp[c, i + 2 + reach] - here)
                basis[1, c, i + 2] = push

        def apply(k, carry):
            for c in range(2):
                edge_up[k, c] = basis[k + 1, c, pl.ds(2, sections), 0, :]
                edge_dn[k, c] = basis[k + 1, c, pl.ds(2, sections), n_rows - 1, :]

            @pl.when(jnp.logical_not(first))
            def _():
                to_up(k).start()

            @pl.when(jnp.logical_not(last))
            def _():
                to_dn(k).start()

            @pl.when(jnp.logical_not(first))
            def _():
                to_up(k).wait_send()
                to_dn(k).wait_recv()

            @pl.when(jnp.logical_not(last))
            def _():
                to_dn(k).wait_send()
                to_up(k).wait_recv()

            twice = jnp.where(k == 0, 1.0, 2.0)
            for c in range(2):
                for i in range(sections):
                    x = basis[k + 1, c, i + 2]
                    higher = jnp.concatenate([halo_up[k, c, i : i + 1, :], x[: n_rows - 1]], axis=0)
                    lower = jnp.concatenate([x[1:], halo_dn[k, c, i : i + 1, :]], axis=0)
                    left = jnp.where(column == 0, 0.0, pltpu.roll(x, 1, 1))
                    right = jnp.where(column == width - 1, 0.0, pltpu.roll(x, width - 1, 1))
                    summed = (higher + lower) + (left + right) - diag[i] * x
                    for which, reach in enumerate(REACHES):
                        summed = summed + fields[which, i] * basis[k + 1, c, i + 2 + reach]
                    basis[k + 2, c, i + 2] = twice * (summed * (1.0 / HALF) + x) - basis[k, c, i + 2]
            return carry

        lax.fori_loop(0, FIRE_STEPS - 1, apply, 0)

        pairs = [(j, k) for j in range(FIRE_STEPS) for k in range(j, FIRE_STEPS)]

        def products(i, carry):
            for c in range(2):
                for part in range(width // LANES):
                    own_k = [basis[k + 1, c, i + 2, :, part * LANES : (part + 1) * LANES] for k in range(FIRE_STEPS)]
                    carry = tuple(a + own_k[j] * own_k[k] for a, (j, k) in zip(carry, pairs))
            return carry

        zero = jnp.zeros((n_rows, LANES), jnp.float32)
        sums = lax.fori_loop(0, sections, products, tuple(zero for _ in pairs))
        for value, (j, k) in zip(sums, pairs):
            line = jnp.sum(value, axis=0, keepdims=True)
            rows[8 * j + k : 8 * j + k + 1, :] = line
            if j != k:
                rows[8 * k + j : 8 * k + j + 1, :] = line
        dots = jnp.sum(rows[...], axis=1, keepdims=True)
        local = jnp.zeros((8, LANES), jnp.float32)
        for j in range(FIRE_STEPS):
            local = jnp.where(lane == j, dots[8 * j : 8 * j + 8], local)
        gram[outer, 0] = local
        matrix = all_sum(outer)

        def force_row(v):
            before = jnp.where(lane == 0, 0.0, pltpu.roll(v, 1, 1))
            after = jnp.where(lane == LANES - 1, 0.0, pltpu.roll(v, LANES - 1, 1))
            return HALF * (0.5 * (before + after) + jnp.where(lane == 1, 0.5 * before, 0.0) - v)

        def force_col(v):
            before = jnp.where(sub == 0, 0.0, pltpu.roll(v, 1, 0))
            after = jnp.where(sub == 7, 0.0, pltpu.roll(v, 7, 0))
            return HALF * (0.5 * (before + after) + jnp.where(sub == 1, 0.5 * before, 0.0) - v)

        def square(row, col):
            parts = jnp.sum(matrix * row * col, axis=1, keepdims=True)
            return jnp.maximum(jnp.sum(parts, axis=0, keepdims=True), 0.0)

        f_row, f_col = (lane == 0).astype(jnp.float32), (sub == 0).astype(jnp.float32)
        v_row, v_col = jnp.zeros_like(f_row), jnp.zeros_like(f_row)
        gain = jnp.zeros_like(f_row)
        for step in range(FIRE_STEPS):
            h = steps[outer, step]
            v_row, v_col = v_row + h * f_row, v_col + h * f_col
            vv, ff = square(v_row, v_col), square(f_row, f_col)
            ratio = jnp.sqrt(vv + EPSILON) / jnp.sqrt(ff + EPSILON)
            limit = jnp.minimum(1.0, SPEED_CAP / jnp.sqrt(vv * (1.0 / node_total) + EPSILON))
            scale = limit * keep[outer, step]
            mix = MIXING * ratio
            v_row = scale * ((1.0 - MIXING) * v_row + mix * f_row)
            v_col = scale * ((1.0 - MIXING) * v_col + mix * f_col)
            gain = gain + h * v_col
            if step < FIRE_STEPS - 1:
                f_row, f_col = f_row + h * force_row(v_row), f_col + h * force_col(v_col)
        wide = [
            jnp.broadcast_to(jnp.concatenate([gain[k : k + 1]] * (width // LANES), axis=1), (n_rows, width))
            for k in range(FIRE_STEPS)
        ]
        for c in range(2):
            for i in range(sections):
                moved = disp[c, i + 2]
                for k in range(FIRE_STEPS):
                    moved = moved + wide[k] * basis[k + 1, c, i + 2]
                disp[c, i + 2] = moved

    def send_out(j):
        peer = lax.rem(s + j, n_sec)
        return pltpu.make_async_remote_copy(
            src_ref=disp.at[:, pl.ds(2 + peer * own, own)], dst_ref=out.at[:, :, q],
            send_sem=out_send.at[j], recv_sem=out_recv.at[j], device_id=(peer, t), device_id_type=MESH)

    for j in range(1, n_sec):
        send_out(j).start()
    mine = pltpu.make_async_copy(disp.at[:, pl.ds(2 + s * own, own)], out.at[:, :, q], out_recv.at[0])
    mine.start()
    mine.wait()
    for j in range(1, n_sec):
        send_out(j).wait()


def relax(packed, steps, keep, n_sec, n_tile):
    _, own, _, n_rows, width = packed.shape
    sections = own * n_sec
    f32 = jnp.float32
    dma = pltpu.SemaphoreType.DMA
    vmem = pl.BlockSpec(memory_space=pltpu.VMEM)
    smem = pl.BlockSpec(memory_space=pltpu.SMEM)
    hops = FIRE_STEPS - 1
    edges = pltpu.VMEM((hops, 2, sections, width), f32)
    return pl.pallas_call(
        functools.partial(fire_kernel, n_sec, n_tile),
        out_shape=jax.ShapeDtypeStruct((2,) + packed.shape[1:], f32),
        in_specs=[smem, smem, vmem],
        out_specs=vmem,
        scratch_shapes=[
            pltpu.VMEM((8, sections, n_rows, width), f32),
            pltpu.VMEM((2, sections + 4, n_rows, width), f32),
            pltpu.VMEM((FIRE_STEPS + 1, 2, sections + 4, n_rows, width), f32),
            pltpu.VMEM((sections, n_rows, width), f32),
            edges, edges, edges, edges,
            pltpu.VMEM((64, LANES), f32),
            pltpu.VMEM((OUTER, 2, 8, LANES), f32),
            pltpu.VMEM((OUTER, n_sec, 8, LANES), f32),
            pltpu.VMEM((OUTER, n_tile, 8, LANES), f32),
            dma((n_sec,)), dma((n_sec,)),
            dma((hops,)), dma((hops,)), dma((hops,)), dma((hops,)),
            dma((OUTER, n_sec)), dma((OUTER, n_sec)), dma((OUTER, n_tile)), dma((OUTER, n_tile)),
            dma((n_sec,)), dma((n_sec,)),
        ],
        compiler_params=pltpu.CompilerParams(collective_id=0, has_side_effects=True),
        cost_estimate=pl.CostEstimate(flops=10**9, bytes_accessed=2 * 10**8, transcendentals=0),
        name="relax",
    )(steps, keep, packed)


def copy_block(index, source, target):
    target[...] = source[...]


def place_blocks(blocks, index):
    count = index.shape[0]
    side = blocks.shape[1:]
    return pl.pallas_call(
        copy_block,
        grid_spec=pltpu.PrefetchScalarGridSpec(
            num_scalar_prefetch=1, grid=(count,),
            in_specs=[pl.BlockSpec((1,) + side, lambda i, at: (at[i], 0, 0))],
            out_specs=pl.BlockSpec((1,) + side, lambda i, at: (i, 0, 0)),
        ),
        out_shape=jax.ShapeDtypeStruct((count,) + side, jnp.float32),
        name="place",
    )(index, blocks)


def pick_kernel(anchor, source, target):
    lane = lax.broadcasted_iota(jnp.int32, (1, source.shape[2]), 1)
    for b in range(target.shape[1]):
        node = anchor[b]
        for c in range(2):
            line = source[c, pl.ds(node // source.shape[2], 1), :]
            value = jnp.sum(jnp.where(lane == node % source.shape[2], line, 0.0), axis=1, keepdims=True)
            target[c, b : b + 1, :] = jnp.broadcast_to(value, (1, LANES))


def pick_nodes(field, anchor):
    return pl.pallas_call(
        pick_kernel,
        out_shape=jax.ShapeDtypeStruct((2, anchor.shape[0], LANES), jnp.float32),
        in_specs=[pl.BlockSpec(memory_space=pltpu.SMEM), pl.BlockSpec(memory_space=pltpu.VMEM)],
        out_specs=pl.BlockSpec(memory_space=pltpu.VMEM),
        name="pick",
    )(anchor, field)[:, :, 0]


def split_dot(a, b, dims):
    a_hi, b_hi = a.astype(jnp.bfloat16), b.astype(jnp.bfloat16)
    a_lo = (a - a_hi.astype(jnp.float32)).astype(jnp.bfloat16)
    b_lo = (b - b_hi.astype(jnp.float32)).astype(jnp.bfloat16)
    dot = functools.partial(lax.dot_general, dimension_numbers=dims, preferred_element_type=jnp.float32)
    return dot(a_hi, b_hi) + (dot(a_hi, b_lo) + dot(a_lo, b_hi))


def render_kernel(slot, shift, blocks, spans):
    item = pl.program_id(0)

    @pl.when(item == 0)
    def _():
        spans[...] = jnp.zeros_like(spans)

    chosen = slot[item]

    @pl.when(chosen >= 0)
    def _():
        side, size = blocks.shape[1], spans.shape[1]
        y, x = shift[2 * item], shift[2 * item + 1]
        out_at = lax.broadcasted_iota(jnp.int32, (size, side), 0)
        in_at = lax.broadcasted_iota(jnp.int32, (size, side), 1)
        apart = (out_at - in_at).astype(jnp.float32)
        row_hats = jnp.maximum(0.0, 1.0 - jnp.abs(apart - y))
        col_hats = jnp.maximum(0.0, 1.0 - jnp.abs(apart - x))
        halfway = split_dot(blocks[0], col_hats, (((1,), (1,)), ((), ())))
        drawn = split_dot(row_hats, halfway, (((1,), (0,)), ((), ())))
        spans[chosen] = spans[chosen] + drawn


def render(blocks, slot, shift):
    count, side, _ = blocks.shape
    return pl.pallas_call(
        render_kernel,
        grid_spec=pltpu.PrefetchScalarGridSpec(
            num_scalar_prefetch=2, grid=(count,),
            in_specs=[pl.BlockSpec((1, side, side), lambda i, *_: (i, 0, 0))],
            out_specs=pl.BlockSpec((SPAN_DEV, CH, CH), lambda i, *_: (0, 0, 0)),
        ),
        out_shape=jax.ShapeDtypeStruct((SPAN_DEV, CH, CH), jnp.float32),
        name="render",
    )(slot, shift, blocks)


def body(
    n_sec, n_tile,
    displacement, coupling, matches, step_sizes, restarts, images,
    block_anchor, block_dest, block_slot, block_offset, block_count,
):
    own, tile_rows, width = displacement.shape[1:]
    tiles = n_tile

    blocks_here = block_anchor.shape[1]
    owners = block_dest[0, :, 0]
    capacity = max(2, 2 * blocks_here // tiles)
    owner_hot = (owners[:, None] == jnp.arange(tiles)[None, :]).astype(jnp.int32)
    rank_all = jnp.cumsum(owner_hot, axis=0) - owner_hot
    position = owners * capacity + jnp.sum(rank_all * owner_hot, axis=1)
    placer = position[None, :] == jnp.arange(tiles * capacity)[:, None]
    held = jnp.arange(blocks_here, dtype=jnp.int32)
    block_of = jnp.sum(jnp.where(placer, held[None, :], 0), axis=1)
    send_blocks = place_blocks(images[0], block_of)
    blocks_in = lax.all_to_all(send_blocks, "tile", split_axis=0, concat_axis=0, tiled=True)

    section = lax.axis_index("sec") * own + jnp.arange(own)
    reach = jnp.array(REACHES, jnp.int32)[:, None]
    valid = (section[None] + reach >= 0) & (section[None] + reach < own * n_sec)
    springs = jnp.where(valid[:, :, None, None], coupling, 0.0)
    pull = jnp.sum(springs[:, None] * matches, axis=0)
    packed = jnp.concatenate([springs, pull, displacement], axis=0)
    packed = packed.reshape(8, own, n_sec, tile_rows // n_sec, width)
    keep = 1.0 - restarts.astype(jnp.float32)
    aligned = relax(packed, step_sizes, keep, n_sec, n_tile)
    aligned = aligned.reshape(displacement.shape)

    moved = pick_nodes(aligned.reshape(2, own * tile_rows, width), block_anchor[0])
    shifts = block_offset[0].astype(jnp.float32) + moved.T
    target = jnp.where(held < block_count[0, 0], block_slot[0] + 1, 0).astype(jnp.float32)
    small = jnp.concatenate([shifts, target[:, None], jnp.zeros_like(target)[:, None]], axis=1)
    send_small = jnp.sum(jnp.where(placer[:, :, None], small[None], 0.0), axis=1)
    send_small, blocks_in = lax.optimization_barrier((send_small, blocks_in))
    small_in = lax.all_to_all(send_small, "tile", split_axis=0, concat_axis=0, tiled=True)
    slot = small_in[:, 2].astype(jnp.int32) - 1
    spans = render(blocks_in, slot, small_in[:, :2].reshape(-1))
    return (aligned, spans)


def solution(mesh):
    placed = (
        P(None, "sec", "tile", None),
        P(None, "sec", "tile", None),
        P(None, None, "sec", "tile", None),
        P(),
        P(),
        P("sec", "tile", None, None),
        P("sec", "tile"),
        P("sec", "tile", None),
        P("sec", "tile"),
        P("sec", "tile", None),
        P("sec", "tile"),
    )
    return jax.shard_map(
        functools.partial(body, mesh.shape["sec"], mesh.shape["tile"]),
        mesh=mesh,
        in_specs=placed,
        out_specs=(P(None, "sec", "tile", None), P(("sec", "tile"), None, None)),
        check_vma=False,
    )
```
